512 devices in a mesh: seq: 64 (over z, x, core), head: 8 (over y).
Axes of the slice: x: 4, y: 8, z: 8, core: 2. Of those that a mesh axis runs over, the one named last changes fastest.
Arguments:
- query_rows: bfloat16 [8192, 8192], P('seq', 'head'), may hold values from -6 to 6
- key_rows: bfloat16 [8192, 8192], P('seq', 'head'), may hold values from -6 to 6
- value_rows: bfloat16 [8192, 8192], P('seq', 'head'), may hold values from -6 to 6
- grad_output: bfloat16 [8192, 8192], P('seq', 'head'), may hold values from -6 to 6
- norm_gain: float32 [8192], P('head'), may hold values from 0.5 to 1.5
Outputs:
- grad_query: bfloat16 [8192, 8192], P('seq', 'head')
- grad_key: bfloat16 [8192, 8192], P('seq', 'head')
- grad_value: bfloat16 [8192, 8192], P('seq', 'head')
- grad_gain: float32 [8192], P('head')
The draws below stay inside these ranges and needn't reach their ends.
All inputs are finite; a program needn't handle non-finite values.
Results may differ from the reference program's by a relative error of at most 0.0031.
Values sent between devices are 32-bit elements; how exact they have to be, the bound alone decides.
No kernel may reach another device: no remote copies, remote signals or barrier semaphores. Data moves between devices by JAX's collectives and lax.ppermute only.
A program may use at most 128 MiB of HBM per device.

```python
import jax
import jax.numpy as jnp
from jax import lax

HEADS = 64
DH = 128
TOK_DEV = 128
W = 8192
TOKENS = 8192


def levels(stream_key, extent, shards, least, largest):
    factor_of = 1.0
    for axis_at, shards_of in shards:
        steps = jax.random.uniform(jax.random.fold_in(jax.random.fold_in(stream_key, 6), axis_at), (shards_of,), jnp.float32, least / len(shards), largest / len(shards))
        factor_of = factor_of * jnp.repeat(jnp.exp(steps), extent[axis_at] // shards_of).reshape((-1,) + (1,) * (len(extent) - 1 - axis_at))
    return factor_of


def scatter_about(stream_key, extent, spread, reach, pieces=(), kind=jnp.bfloat16):
    entries = spread * jax.random.normal(stream_key, extent, jnp.float32)
    if pieces:
        entries = entries * levels(stream_key, extent, pieces, -0.22, 0.18)
    return jnp.clip(entries, -reach, reach).astype(kind)


def setup_inputs(seed: int = 0) -> dict:
    arg_keys = jax.random.split(jax.random.key(seed), 6)
    query_rows = scatter_about(arg_keys[0], (TOKENS, W), 1.0, 6.0, ((0, 64), (1, 8)))
    key_rows = scatter_about(arg_keys[1], (TOKENS, W), 1.0, 6.0, ((0, 64), (1, 8)))
    value_rows = scatter_about(arg_keys[2], (TOKENS, W), 1.0, 6.0, ((0, 64), (1, 8)))
    grad_output = scatter_about(arg_keys[3], (TOKENS, W), 1.0, 6.0, ((0, 64), (1, 8)))
    norm_gain = jnp.clip(1.0 + 0.1 * jax.random.normal(arg_keys[4], (W,), jnp.float32), 0.5, 1.5)
    return dict(query_rows=query_rows, key_rows=key_rows, value_rows=value_rows, grad_output=grad_output, norm_gain=norm_gain)


epsilon = 1e-06
highest = lax.Precision.HIGHEST

def causal_of(count):
    upper = lax.broadcasted_iota(jnp.int32, (count, count), 0)
    lower = lax.broadcasted_iota(jnp.int32, (count, count), 1)
    return upper >= lower

def reference(query_rows, key_rows, value_rows, grad_output, norm_gain):
    blocks = TOKENS // TOK_DEV
    query_blocks = query_rows.reshape(blocks, TOK_DEV, HEADS, DH)
    key_blocks = key_rows.reshape(blocks, TOK_DEV, HEADS, DH)
    value_blocks = value_rows.reshape(blocks, TOK_DEV, HEADS, DH)
    grad_blocks = grad_output.reshape(blocks, TOK_DEV, W)
    causal = causal_of(TOK_DEV)[None]
    gain_float = norm_gain.astype(jnp.float32)

    def forward_block(carry, block):
        state, gain_total = carry
        query_block, key_block, value_block, grad_block = block
        query_float = query_block.astype(jnp.float32)
        key_float = key_block.astype(jnp.float32)
        value_float = value_block.astype(jnp.float32)
        scores = jnp.einsum('thd,shd->hts', query_float, key_float, precision=highest)
        probs = jnp.where(causal, scores, 0.0).astype(jnp.bfloat16)
        attn = jnp.einsum('hts,she->the', probs.astype(jnp.float32), value_float, precision=highest)
        attn = attn + jnp.einsum('thd,hde->the', query_float, state, precision=highest)
        flat = attn.reshape(TOK_DEV, W)
        grad_float = grad_block.astype(jnp.float32)
        scaled = grad_float * gain_float[None, :]
        square = lax.optimization_barrier(jnp.sum(flat * flat, axis=1))
        inverse = lax.rsqrt(square / W + epsilon)
        normed = flat * inverse[:, None]
        cross = lax.optimization_barrier(jnp.sum(scaled * normed, axis=1))
        grad_attn = inverse[:, None] * (scaled - normed * (cross / W)[:, None])
        gain_total = gain_total + lax.optimization_barrier(jnp.sum(grad_float * normed, axis=0))
        grad_heads = grad_attn.reshape(TOK_DEV, HEADS, DH)
        grad_round = grad_heads.astype(jnp.bfloat16).astype(jnp.float32)
        dprobs = jnp.einsum('the,she->hts', grad_round, value_float, precision=highest)
        dprobs = jnp.where(causal, dprobs, 0.0).astype(jnp.bfloat16).astype(jnp.float32)
        grad_query = jnp.einsum('hts,shd->thd', dprobs, key_float, precision=highest)
        grad_query = grad_query + jnp.einsum('the,hde->thd', grad_heads, state, precision=highest)
        state = state + jnp.einsum('thd,the->hde', key_float, value_float, precision=highest)
        return ((state, gain_total), (grad_query.astype(jnp.bfloat16).reshape(TOK_DEV, W), grad_attn))
    start_state = jnp.zeros((HEADS, DH, DH), jnp.float32)
    start_gain = jnp.zeros((W,), jnp.float32)
    (final_state, grad_gain), (grad_query, grad_attn) = lax.scan(forward_block, (start_state, start_gain), (query_blocks, key_blocks, value_blocks, grad_blocks))

    def reverse_block(later, block):
        query_block, key_block, value_block, grad_block = block
        query_float = query_block.astype(jnp.float32)
        key_float = key_block.astype(jnp.float32)
        value_float = value_block.astype(jnp.float32)
        scores = jnp.einsum('thd,shd->hts', query_float, key_float, precision=highest)
        probs = jnp.where(causal, scores, 0.0).astype(jnp.bfloat16).astype(jnp.float32)
        grad_heads = grad_block.reshape(TOK_DEV, HEADS, DH)
        grad_round = grad_heads.astype(jnp.bfloat16).astype(jnp.float32)
        dprobs = jnp.einsum('the,she->hts', grad_round, value_float, precision=highest)
        dprobs = jnp.where(causal, dprobs, 0.0).astype(jnp.bfloat16).astype(jnp.float32)
        grad_key = jnp.einsum('hts,thd->shd', dprobs, query_float, precision=highest)
        grad_key = grad_key + jnp.einsum('she,hde->shd', value_float, later, precision=highest)
        grad_value = jnp.einsum('hts,the->she', probs, grad_round, precision=highest)
        grad_value = grad_value + jnp.einsum('shd,hde->she', key_float, later, precision=highest)
        later = later + jnp.einsum('thd,the->hde', query_float, grad_heads, precision=highest)
        return (later, (grad_key.astype(jnp.bfloat16).reshape(TOK_DEV, W), grad_value.astype(jnp.bfloat16).reshape(TOK_DEV, W)))
    final_later, (grad_key, grad_value) = lax.scan(reverse_block, start_state, (query_blocks, key_blocks, value_blocks, grad_attn), reverse=True)
    return (grad_query.reshape(TOKENS, W), grad_key.reshape(TOKENS, W), grad_value.reshape(TOKENS, W), grad_gain)
```

```python
import functools

import jax
import jax.numpy as jnp
from jax import lax
from jax.experimental import pallas as pl
from jax.experimental.pallas import tpu as pltpu
from jax.sharding import Mesh, PartitionSpec as P

DH = 128
EPS = 1e-06
F32 = jnp.float32
BF16 = jnp.bfloat16


def dot(a, b, ca, cb):
    return lax.dot_general(a, b, (((ca,), (cb,)), ((), ())), preferred_element_type=F32)


def split(x):
    hi = x.astype(BF16)
    return hi, (x - hi.astype(F32)).astype(BF16)


def causal():
    rows = lax.broadcasted_iota(jnp.int32, (DH, DH), 0)
    cols = lax.broadcasted_iota(jnp.int32, (DH, DH), 1)
    return rows >= cols


def hs(h):
    return slice(h * DH, (h + 1) * DH)


def whole(shape):
    return pl.BlockSpec(shape, lambda i, c: (0,) * len(shape))


def call(name, body, core, ins, in_specs, outs, out_specs=None, scratch=()):
    if out_specs is None:
        out_specs = [whole(o.shape) for o in outs]
    return pl.pallas_call(
        body,
        name=name,
        out_shape=outs,
        grid_spec=pltpu.PrefetchScalarGridSpec(
            num_scalar_prefetch=1,
            grid=(1,),
            in_specs=in_specs,
            out_specs=out_specs,
            scratch_shapes=list(scratch),
        ),
    )(core, *ins)


def sds(shape, dtype):
    return jax.ShapeDtypeStruct(shape, dtype)


def send_body(c, q, k, v, g, out):
    for i, ref in enumerate((q, k, v, g)):
        out[i] = ref[...].astype(F32)


def state_body(c, q, k, v, g, got, rows, first, total):
    mine = pl.multiple_of(c[0] * DH, DH)
    other = pl.multiple_of((1 - c[0]) * DH, DH)
    for i, ref in enumerate((q, k, v, g)):
        rows[i, pl.ds(mine, DH), :] = ref[...]
        rows[i, pl.ds(other, DH), :] = got[i].astype(BF16)
    for h in range(first.shape[0]):
        s0 = dot(rows[1, 0:DH, hs(h)], rows[2, 0:DH, hs(h)], 0, 0)
        s1 = dot(rows[1, DH : 2 * DH, hs(h)], rows[2, DH : 2 * DH, hs(h)], 0, 0)
        first[h] = s0
        total[hs(h), :] = s0 + s1


def local_body(c, rows, probs, intra):
    mask = causal()
    heads = probs.shape[1]
    for b in range(2):
        r = slice(b * DH, (b + 1) * DH)
        for h in range(heads):
            p = dot(rows[0, r, hs(h)], rows[1, r, hs(h)], 1, 1)
            p = jnp.where(mask, p, 0.0).astype(BF16)
            probs[b, h] = p
            intra[r, hs(h)] = dot(p, rows[2, r, hs(h)], 1, 0)


def earlier_body(n, c, x, out):
    share = x.shape[0] // n
    acc = jnp.zeros((share, DH), F32)
    for i in range(n):
        out[i * share : (i + 1) * share, :] = acc
        if i + 1 < n:
            acc = acc + x[i * share : (i + 1) * share, :]


def attn_body(c, rows, intra, first, prior, gain, flat, parts):
    heads = first.shape[0]
    for b in range(2):
        r = slice(b * DH, (b + 1) * DH)
        square = jnp.zeros((DH, DH), F32)
        cross = jnp.zeros((DH, DH), F32)
        for h in range(heads):
            p = prior[hs(h), :]
            if b == 1:
                p = p + first[h]
            hi, lo = split(p)
            q = rows[0, r, hs(h)]
            f = intra[r, hs(h)] + (dot(q, lo, 1, 0) + dot(q, hi, 1, 0))
            flat[r, hs(h)] = f
            square = square + f * f
            cross = cross + (rows[3, r, hs(h)].astype(F32) * gain[:, hs(h)]) * f
        sq = jnp.sum(square.T, axis=0, keepdims=True)
        cr = jnp.sum(cross.T, axis=0, keepdims=True)
        for j in range(parts.shape[0]):
            parts[j, b : b + 1, :] = sq
            parts[j, 2 + b : 3 + b, :] = cr


def grad_body(n, width, c, rows, flat, gain, parts, gd, second, out):
    heads = second.shape[0]
    own = heads * DH // n
    total = jnp.sum(parts[...], axis=0)
    gain_rows = [jnp.zeros((1, DH), F32) for _ in range(heads)]
    sums = [None] * heads
    for b in range(2):
        r = slice(b * DH, (b + 1) * DH)
        inverse = lax.rsqrt(total[b : b + 1, :] / width + EPS)
        scale = inverse * total[2 + b : 3 + b, :] / width
        inverse = jnp.broadcast_to(inverse, (DH, DH)).T
        scale = jnp.broadcast_to(scale, (DH, DH)).T
        for h in range(heads):
            g = rows[3, r, hs(h)].astype(F32)
            normed = flat[r, hs(h)] * inverse
            d = inverse * (g * gain[:, hs(h)] - normed * scale)
            gd[r, hs(h)] = d
            gain_rows[h] = gain_rows[h] + jnp.sum(g * normed, axis=0, keepdims=True)
            hi, lo = split(d)
            q = rows[0, r, hs(h)]
            s = dot(q, lo, 0, 0) + dot(q, hi, 0, 0)
            if b == 1:
                second[h] = s
                sums[h] = sums[h] + s
            else:
                sums[h] = s
    for j in range(n):
        h, at = divmod(j * own, DH)
        out[j * (own + 1) : j * (own + 1) + own, :] = sums[h][at : at + own, :]
        out[j * (own + 1) + own : (j + 1) * (own + 1), :] = gain_rows[j % heads]


def query_body(c, rows, probs, gd, prior, first, gq, gk, gv):
    mask = causal()
    heads = first.shape[0]
    for b in range(2):
        r = slice(b * DH, (b + 1) * DH)
        for h in range(heads):
            q, k, v = rows[0, r, hs(h)], rows[1, r, hs(h)], rows[2, r, hs(h)]
            hi, lo = split(gd[r, hs(h)])
            dp = dot(hi, v, 1, 1)
            dp = jnp.where(mask, dp, 0.0).astype(BF16)
            p = prior[hs(h), :]
            if b == 1:
                p = p + first[h]
            phi, plo = split(p)
            t = dot(lo, phi, 1, 1) + dot(hi, plo, 1, 1) + dot(hi, phi, 1, 1)
            gq[r, hs(h)] = dot(dp, k, 1, 0) + t
            gk[r, hs(h)] = dot(dp, q, 0, 0)
            gv[r, hs(h)] = dot(probs[b, h], hi, 0, 0)


def later_body(n, c, x, out):
    share = x.shape[0] // n
    own = share - 1
    acc = jnp.zeros((own, DH), F32)
    gain = jnp.zeros((1, DH), F32)
    for i in range(n):
        gain = gain + x[i * share + own : (i + 1) * share, :]
    for i in reversed(range(n)):
        out[i * share : i * share + own, :] = acc
        out[i * share + own : (i + 1) * share, :] = gain
        if i:
            acc = acc + x[i * share : i * share + own, :]


def key_body(n, c, rows, gq, gk, gv, second, got, keep, send, later):
    heads = second.shape[0]
    own = heads * DH // n
    for j in range(n):
        later[j * own : (j + 1) * own, :] = got[j * (own + 1) : j * (own + 1) + own, :]
    mine = pl.multiple_of(c[0] * DH, DH)
    other = pl.multiple_of((1 - c[0]) * DH, DH)
    keep[0] = gq[pl.ds(mine, DH), :]
    send[0:DH, :] = gq[pl.ds(other, DH), :]
    for h in range(heads):
        send[3 * DH : 3 * DH + 8, hs(h)] = jnp.broadcast_to(
            got[h * (own + 1) + own : (h + 1) * (own + 1), :], (8, DH)
        )
        one = later[hs(h), :]
        zero_hi, zero_lo = split(one + second[h])
        one_hi, one_lo = split(one)

        def put(b, kept, sent, hi, lo):
            r = slice(b * DH, (b + 1) * DH)
            k, v = rows[1, r, hs(h)], rows[2, r, hs(h)]
            dk = gk[r, hs(h)] + (dot(v, lo, 1, 1) + dot(v, hi, 1, 1))
            dv = gv[r, hs(h)] + (dot(k, lo, 1, 0) + dot(k, hi, 1, 0))
            if kept is not None:
                kept[1, :, hs(h)] = dk
                kept[2, :, hs(h)] = dv
            else:
                sent[DH : 2 * DH, hs(h)] = dk
                sent[2 * DH : 3 * DH, hs(h)] = dv

        @pl.when(c[0] == 0)
        def _():
            put(0, keep, None, zero_hi, zero_lo)
            put(1, None, send, one_hi, one_lo)

        @pl.when(c[0] == 1)
        def _():
            put(0, None, send, zero_hi, zero_lo)
            put(1, keep, None, one_hi, one_lo)


def final_body(c, keep, gain_keep, got, gq, gk, gv, gain):
    half = keep.shape[2]

    def put(at, away):
        for i, ref in enumerate((gq, gk, gv)):
            ref[:, at : at + half] = keep[i].astype(BF16)
            ref[:, away : away + half] = got[i * DH : (i + 1) * DH, :].astype(BF16)
        gain[:, at : at + half] = gain_keep[0:1, :]
        gain[:, away : away + half] = got[3 * DH : 3 * DH + 1, :]

    @pl.when(c[0] == 0)
    def _():
        put(0, half)

    @pl.when(c[0] == 1)
    def _():
        put(half, 0)


def shards(query_rows, key_rows, value_rows, grad_output, norm_gain):
    count, width = query_rows.shape
    half = width // 2
    heads = half // DH
    both = 2 * count
    chips = lax.axis_size("chip")
    columns = lax.axis_size("head")
    full = columns * width
    at = lax.axis_index("core")
    core = at.astype(jnp.int32).reshape(1)
    swap = [(0, 1), (1, 0)]
    args = (query_rows, key_rows, value_rows, grad_output)
    gains = norm_gain.reshape(1, width)
    mine = pl.BlockSpec((count, half), lambda i, c: (0, c[0]))
    away = pl.BlockSpec((count, half), lambda i, c: (0, 1 - c[0]))
    my_gain = pl.BlockSpec((1, half), lambda i, c: (0, c[0]))
    rows_s = sds((4, both, half), BF16)
    act = sds((both, half), F32)
    state = sds((heads, DH, DH), F32)
    flat_state = sds((heads * DH, DH), F32)
    padded = sds((heads * DH + chips, DH), F32)
    w_rows, w_act, w_state = whole(rows_s.shape), whole(act.shape), whole(state.shape)
    w_flat, w_pad = whole(flat_state.shape), whole(padded.shape)

    def exchange(x):
        y = lax.all_to_all(
            x.reshape(chips, 1, -1), "chip", split_axis=0, concat_axis=0, tiled=True
        )
        return y.reshape(x.shape)

    sent = call("send", send_body, core, args, [away] * 4, [sds((4, count, half), F32)])[0]
    got = lax.ppermute(sent, "core", swap)
    rows, first, total = call(
        "state", state_body, core, (*args, got), [mine] * 4 + [whole(got.shape)],
        [rows_s, state, flat_state],
    )
    mine_states = exchange(total)
    probs, intra = call(
        "local", local_body, core, (rows,), [w_rows],
        [sds((2, heads, DH, DH), BF16), act],
    )
    sums = call(
        "earlier", functools.partial(earlier_body, chips), core, (mine_states,), [w_flat],
        [flat_state],
    )[0]
    prior = exchange(sums)
    group = 2 * columns
    flat, parts = call(
        "attn", attn_body, core, (rows, intra, first, prior, gains),
        [w_rows, w_act, w_state, w_flat, my_gain],
        [act, sds((group, 4, DH), F32)],
    )
    parts = lax.all_to_all(parts, ("core", "head"), split_axis=0, concat_axis=0, tiled=True)
    gd, second, block = call(
        "grad", functools.partial(grad_body, chips, full), core,
        (rows, flat, gains, parts),
        [w_rows, w_act, my_gain, whole(parts.shape)],
        [act, state, padded],
    )
    mine_grads = exchange(block)
    gq, gk, gv = call(
        "query", query_body, core, (rows, probs, gd, prior, first),
        [w_rows, whole(probs.shape), w_act, w_flat, w_state],
        [act, act, act],
    )
    later_sums = call(
        "later", functools.partial(later_body, chips), core, (mine_grads,), [w_pad], [padded]
    )[0]
    later = exchange(later_sums)
    keep, send = call(
        "key", functools.partial(key_body, chips), core,
        (rows, gq, gk, gv, second, later),
        [w_rows, w_act, w_act, w_act, w_state, w_pad],
        [sds((3, count, half), F32), sds((3 * count + 8, half), F32)],
        scratch=[pltpu.VMEM(flat_state.shape, F32)],
    )
    back = lax.ppermute(send, "core", swap)
    outs = [sds((count, width), BF16)] * 3 + [sds((1, width), F32)]
    tail = pl.BlockSpec((8, half), lambda i, c: (3 * count // 8, 0))
    gq, gk, gv, gain = call(
        "final", final_body, core, (keep, send, back),
        [whole(keep.shape), tail, whole(back.shape)], outs,
    )
    return gq, gk, gv, gain.reshape(width)


def solution(mesh):
    names = dict(mesh.shape)
    inner = Mesh(
        mesh.devices.reshape(names["seq"] // 2, 2, names["head"]), ("chip", "core", "head")
    )
    seq = ("chip", "core")
    placed = (P(seq, "head"),) * 4 + (P("head"),)
    return jax.shard_map(
        shards,
        mesh=inner,
        in_specs=placed,
        out_specs=(P(seq, "head"),) * 3 + (P("head"),),
        check_vma=False,
    )
```

```python
import functools

import jax
import jax.numpy as jnp
from jax import lax
from jax.experimental import pallas as pl
from jax.experimental.pallas import tpu as pltpu
from jax.sharding import Mesh, PartitionSpec as P

DH = 128
EPS = 1e-06
F32 = jnp.float32
BF16 = jnp.bfloat16


def dot(a, b, ca, cb):
    return lax.dot_general(a, b, (((ca,), (cb,)), ((), ())), preferred_element_type=F32)


def split(x):
    hi = x.astype(BF16)
    return hi, (x - hi.astype(F32)).astype(BF16)


def dot2(a, hi, lo, cb):
    return dot(jnp.concatenate([a, a], 1), jnp.concatenate([hi, lo], cb), 1, cb)


def causal():
    rows = lax.broadcasted_iota(jnp.int32, (DH, DH), 0)
    cols = lax.broadcasted_iota(jnp.int32, (DH, DH), 1)
    return rows >= cols


def hs(h):
    return slice(h * DH, (h + 1) * DH)


def call(name, body, core, ins, outs, scratch=(), far=()):
    vmem = pl.BlockSpec(memory_space=pltpu.VMEM)
    count = len(ins)
    ins = [
        x if i in far else pltpu.with_memory_space_constraint(x, pltpu.VMEM)
        for i, x in enumerate(ins)
    ]
    outs = [
        o if count + i in far else pltpu.VMEM(o.shape, o.dtype) for i, o in enumerate(outs)
    ]
    return pl.pallas_call(
        body,
        name=name,
        out_shape=outs,
        in_specs=[pl.BlockSpec(memory_space=pltpu.SMEM)] + [vmem] * len(ins),
        out_specs=[vmem] * len(outs),
        scratch_shapes=list(scratch),
        compiler_params=pltpu.CompilerParams(vmem_limit_bytes=16 * 2**20),
    )(core, *ins)


def sds(shape, dtype):
    return jax.ShapeDtypeStruct(shape, dtype)


def half_of(ref, at, half):
    return ref[:, pl.ds(pl.multiple_of(at * half, DH), half)]


def send_body(c, q, k, v, g, out):
    for i, ref in enumerate((q, k, v, g)):
        out[i] = half_of(ref, 1 - c[0], out.shape[2]).astype(F32)


def place(c, ref, got, row, out, at):
    mine = pl.multiple_of(c[0] * DH, DH)
    other = pl.multiple_of((1 - c[0]) * DH, DH)
    out[at, pl.ds(mine, DH), :] = half_of(ref, c[0], out.shape[2])
    out[at, pl.ds(other, DH), :] = got[row].astype(BF16)


def state_body(c, k, v, got, kv, first, total):
    place(c, k, got, 1, kv, 0)
    place(c, v, got, 2, kv, 1)
    for h in range(first.shape[0]):
        s0 = dot(kv[0, 0:DH, hs(h)], kv[1, 0:DH, hs(h)], 0, 0)
        s1 = dot(kv[0, DH : 2 * DH, hs(h)], kv[1, DH : 2 * DH, hs(h)], 0, 0)
        first[h] = s0
        total[hs(h), :] = s0 + s1


def local_body(c, q, g, got, kv, qg, probs, intra):
    place(c, q, got, 0, qg, 0)
    place(c, g, got, 3, qg, 1)
    mask = causal()
    heads = probs.shape[1]
    for b in range(2):
        r = slice(b * DH, (b + 1) * DH)
        for h in range(heads):
            p = dot(qg[0, r, hs(h)], kv[0, r, hs(h)], 1, 1)
            p = jnp.where(mask, p, 0.0).astype(BF16)
            probs[b, h] = p
            intra[r, hs(h)] = dot(p, kv[1, r, hs(h)], 1, 0)


def earlier_body(n, c, x, out):
    share = x.shape[0] // n
    acc = jnp.zeros((share, DH), F32)
    for i in range(n):
        out[i * share : (i + 1) * share, :] = acc
        if i + 1 < n:
            acc = acc + x[i * share : (i + 1) * share, :]


def attn_body(c, qg, intra, first, prior, gain, flat, parts):
    heads = first.shape[0]
    my_gain = half_of(gain, c[0], heads * DH)
    for b in range(2):
        r = slice(b * DH, (b + 1) * DH)
        square = jnp.zeros((DH, DH), F32)
        cross = jnp.zeros((DH, DH), F32)
        for h in range(heads):
            p = prior[hs(h), :]
            if b == 1:
                p = p + first[h]
            hi, lo = split(p)
            f = intra[r, hs(h)] + dot2(qg[0, r, hs(h)], hi, lo, 0)
            flat[r, hs(h)] = f
            square = square + f * f
            cross = cross + (qg[1, r, hs(h)].astype(F32) * my_gain[:, hs(h)]) * f
        sq = jnp.sum(square.T, axis=0, keepdims=True)
        cr = jnp.sum(cross.T, axis=0, keepdims=True)
        for j in range(parts.shape[0]):
            parts[j, b : b + 1, :] = sq
            parts[j, 2 + b : 3 + b, :] = cr


def grad_body(n, width, c, qg, flat, gain, parts, gd, second, out):
    heads = second.shape[0]
    own = heads * DH // n
    my_gain = half_of(gain, c[0], heads * DH)
    total = jnp.sum(parts[...], axis=0)
    gain_rows = [jnp.zeros((1, DH), F32) for _ in range(heads)]
    sums = [None] * heads
    for b in range(2):
        r = slice(b * DH, (b + 1) * DH)
        inverse = lax.rsqrt(total[b : b + 1, :] / width + EPS)
        scale = inverse * total[2 + b : 3 + b, :] / width
        inverse = jnp.broadcast_to(inverse, (DH, DH)).T
        scale = jnp.broadcast_to(scale, (DH, DH)).T
        for h in range(heads):
            g = qg[1, r, hs(h)].astype(F32)
            normed = flat[r, hs(h)] * inverse
            d = inverse * (g * my_gain[:, hs(h)] - normed * scale)
            gd[r, hs(h)] = d
            gain_rows[h] = gain_rows[h] + jnp.sum(g * normed, axis=0, keepdims=True)
            hi, lo = split(d)
            q = qg[0, r, hs(h)]
            s = dot(q, lo, 0, 0) + dot(q, hi, 0, 0)
            if b == 1:
                second[h] = s
                sums[h] = sums[h] + s
            else:
                sums[h] = s
    for j in range(n):
        h, at = divmod(j * own, DH)
        out[j * (own + 1) : j * (own + 1) + own, :] = sums[h][at : at + own, :]
        out[j * (own + 1) + own : (j + 1) * (own + 1), :] = gain_rows[j % heads]


def query_body(c, qg, kv, probs, gd, prior, first, gq, gk, gv):
    mask = causal()
    heads = first.shape[0]
    for b in range(2):
        r = slice(b * DH, (b + 1) * DH)
        for h in range(heads):
            q, k, v = qg[0, r, hs(h)], kv[0, r, hs(h)], kv[1, r, hs(h)]
            hi, lo = split(gd[r, hs(h)])
            dp = dot(hi, v, 1, 1)
            dp = jnp.where(mask, dp, 0.0).astype(BF16)
            p = prior[hs(h), :]
            if b == 1:
                p = p + first[h]
            phi, plo = split(p)
            t = dot(lo, phi, 1, 1) + dot2(hi, phi, plo, 1)
            gq[r, hs(h)] = dot(dp, k, 1, 0) + t
            gk[r, hs(h)] = dot(dp, q, 0, 0)
            gv[r, hs(h)] = dot(probs[b, h], hi, 0, 0)


def later_body(n, c, x, out):
    share = x.shape[0] // n
    own = share - 1
    acc = jnp.zeros((own, DH), F32)
    gain = jnp.zeros((1, DH), F32)
    for i in range(n):
        gain = gain + x[i * share + own : (i + 1) * share, :]
    for i in reversed(range(n)):
        out[i * share : i * share + own, :] = acc
        out[i * share + own : (i + 1) * share, :] = gain
        if i:
            acc = acc + x[i * share : i * share + own, :]


def key_body(n, c, kv, gq, gk, gv, second, got, keep, send, later):
    heads = second.shape[0]
    own = heads * DH // n
    for j in range(n):
        later[j * own : (j + 1) * own, :] = got[j * (own + 1) : j * (own + 1) + own, :]
    mine = pl.multiple_of(c[0] * DH, DH)
    other = pl.multiple_of((1 - c[0]) * DH, DH)
    keep[0] = gq[pl.ds(mine, DH), :]
    send[0:DH, :] = gq[pl.ds(other, DH), :]
    for h in range(heads):
        send[3 * DH : 3 * DH + 8, hs(h)] = jnp.broadcast_to(
            got[h * (own + 1) + own : (h + 1) * (own + 1), :], (8, DH)
        )
        one = later[hs(h), :]
        zero_hi, zero_lo = split(one + second[h])
        one_hi, one_lo = split(one)

        def put(b, kept, sent, hi, lo):
            r = slice(b * DH, (b + 1) * DH)
            k, v = kv[0, r, hs(h)], kv[1, r, hs(h)]
            dk = gk[r, hs(h)] + dot2(v, hi, lo, 1)
            dv = gv[r, hs(h)] + dot2(k, hi, lo, 0)
            if kept is not None:
                kept[1, :, hs(h)] = dk
                kept[2, :, hs(h)] = dv
            else:
                sent[DH : 2 * DH, hs(h)] = dk
                sent[2 * DH : 3 * DH, hs(h)] = dv

        @pl.when(c[0] == 0)
        def _():
            put(0, keep, None, zero_hi, zero_lo)
            put(1, None, send, one_hi, one_lo)

        @pl.when(c[0] == 1)
        def _():
            put(0, None, send, zero_hi, zero_lo)
            put(1, keep, None, one_hi, one_lo)


def final_body(c, keep, sent, got, gq, gk, gv, gain):
    half = keep.shape[2]

    def put(at, away):
        for i, ref in enumerate((gq, gk, gv)):
            ref[:, at : at + half] = keep[i].astype(BF16)
            ref[:, away : away + half] = got[i * DH : (i + 1) * DH, :].astype(BF16)
        gain[:, at : at + half] = sent[3 * DH : 3 * DH + 1, :]
        gain[:, away : away + half] = got[3 * DH : 3 * DH + 1, :]

    @pl.when(c[0] == 0)
    def _():
        put(0, half)

    @pl.when(c[0] == 1)
    def _():
        put(half, 0)


def shards(query_rows, key_rows, value_rows, grad_output, norm_gain):
    count, width = query_rows.shape
    half = width // 2
    heads = half // DH
    both = 2 * count
    chips = lax.axis_size("chip")
    columns = lax.axis_size("head")
    full = columns * width
    at = lax.axis_index("core")
    core = at.astype(jnp.int32).reshape(1)
    swap = [(0, 1), (1, 0)]
    args = (query_rows, key_rows, value_rows, grad_output)
    gains = norm_gain.reshape(1, width)
    act = sds((both, half), F32)
    pair = sds((2, both, half), BF16)
    state = sds((heads, DH, DH), F32)
    flat_state = sds((heads * DH, DH), F32)
    padded = sds((heads * DH + chips, DH), F32)

    def exchange(x):
        y = lax.all_to_all(
            x.reshape(chips, 1, -1), "chip", split_axis=0, concat_axis=0, tiled=True
        )
        return y.reshape(x.shape)

    sent = call("send", send_body, core, args, [sds((4, count, half), F32)], far=(0, 3))[0]
    got = lax.ppermute(sent, "core", swap)
    kv, first, total = call(
        "state", state_body, core, (key_rows, value_rows, got), [pair, state, flat_state]
    )
    mine_states = exchange(total)
    qg, probs, intra = call(
        "local", local_body, core, (query_rows, grad_output, got, kv),
        [pair, sds((2, heads, DH, DH), BF16), act], far=(0, 1, 5),
    )
    sums = call(
        "earlier", functools.partial(earlier_body, chips), core, (mine_states,), [flat_state]
    )[0]
    prior = exchange(sums)
    flat, parts = call(
        "attn", attn_body, core, (qg, intra, first, prior, gains),
        [act, sds((2 * columns, 4, DH), F32)],
    )
    parts = lax.all_to_all(parts, ("core", "head"), split_axis=0, concat_axis=0, tiled=True)
    gd, second, block = call(
        "grad", functools.partial(grad_body, chips, full), core, (qg, flat, gains, parts),
        [act, state, padded],
    )
    mine_grads = exchange(block)
    gq, gk, gv = call(
        "query", query_body, core, (qg, kv, probs, gd, prior, first), [act, act, act],
        far=(2,),
    )
    later_sums = call(
        "later", functools.partial(later_body, chips), core, (mine_grads,), [padded]
    )[0]
    later = exchange(later_sums)
    keep, send = call(
        "key", functools.partial(key_body, chips), core, (kv, gq, gk, gv, second, later),
        [sds((3, count, half), F32), sds((3 * count + 8, half), F32)],
        scratch=[pltpu.VMEM(flat_state.shape, F32)],
    )
    back = lax.ppermute(send, "core", swap)
    gq, gk, gv, gain = call(
        "final", final_body, core, (keep, send, back),
        [sds((count, width), BF16)] * 3 + [sds((1, width), F32)], far=(3, 4, 5, 6),
    )
    return gq, gk, gv, gain.reshape(width)


def solution(mesh):
    names = dict(mesh.shape)
    inner = Mesh(
        mesh.devices.reshape(names["seq"] // 2, 2, names["head"]), ("chip", "core", "head")
    )
    seq = ("chip", "core")
    placed = (P(seq, "head"),) * 4 + (P("head"),)
    return jax.shard_map(
        shards,
        mesh=inner,
        in_specs=placed,
        out_specs=(P(seq, "head"),) * 3 + (P("head"),),
        check_vma=False,
    )
```

```python
import functools

import jax
import jax.numpy as jnp
from jax import lax
from jax.experimental import pallas as pl
from jax.experimental.pallas import tpu as pltpu
from jax.sharding import Mesh, PartitionSpec as P

DH = 128
EPS = 1e-06
F32 = jnp.float32
BF16 = jnp.bfloat16


def dot(a, b, ca, cb):
    return lax.dot_general(a, b, (((ca,), (cb,)), ((), ())), preferred_element_type=F32)


def split(x):
    hi = x.astype(BF16)
    return hi, (x - hi.astype(F32)).astype(BF16)


def dot2(a, hi, lo, cb):
    return dot(jnp.concatenate([a, a], 1), jnp.concatenate([hi, lo], cb), 1, cb)


def causal():
    rows = lax.broadcasted_iota(jnp.int32, (DH, DH), 0)
    cols = lax.broadcasted_iota(jnp.int32, (DH, DH), 1)
    return rows >= cols


def hs(h):
    return slice(h * DH, (h + 1) * DH)


def call(name, body, core, ins, outs, scratch=(), far=()):
    vmem = pl.BlockSpec(memory_space=pltpu.VMEM)
    count = len(ins)
    ins = [
        x if i in far else pltpu.with_memory_space_constraint(x, pltpu.VMEM)
        for i, x in enumerate(ins)
    ]
    outs = [
        o if count + i in far else pltpu.VMEM(o.shape, o.dtype) for i, o in enumerate(outs)
    ]
    return pl.pallas_call(
        body,
        name=name,
        out_shape=outs,
        in_specs=[pl.BlockSpec(memory_space=pltpu.SMEM)] + [vmem] * len(ins),
        out_specs=[vmem] * len(outs),
        scratch_shapes=list(scratch),
        compiler_params=pltpu.CompilerParams(vmem_limit_bytes=16 * 2**20),
    )(core, *ins)


def sds(shape, dtype):
    return jax.ShapeDtypeStruct(shape, dtype)


def half_of(ref, at, half):
    return ref[:, pl.ds(pl.multiple_of(at * half, DH), half)]


def send_body(c, q, k, v, g, out):
    for i, ref in enumerate((q, k, v, g)):
        out[i] = ref[...].astype(F32)


def place(c, ref, got, row, out, at):
    mine = pl.multiple_of(c[0] * DH, DH)
    other = pl.multiple_of((1 - c[0]) * DH, DH)
    out[at, pl.ds(mine, DH), :] = half_of(ref, c[0], out.shape[2])
    out[at, pl.ds(other, DH), :] = got[row].astype(BF16)


def state_body(c, q, k, v, g, got, qg, kv, total):
    place(c, k, got, 1, kv, 0)
    place(c, v, got, 2, kv, 1)
    for h in range(total.shape[0] // DH):
        total[hs(h), :] = dot(kv[0, :, hs(h)], kv[1, :, hs(h)], 0, 0)
    place(c, q, got, 0, qg, 0)
    place(c, g, got, 3, qg, 1)


def first_state(kv, h):
    return dot(kv[0, 0:DH, hs(h)], kv[1, 0:DH, hs(h)], 0, 0)


def local_body(c, qg, kv, gain, intra, my_gain):
    my_gain[...] = half_of(gain, c[0], my_gain.shape[1])
    mask = causal()
    for h in range(intra.shape[1] // DH):
        hi, lo = split(first_state(kv, h))
        for b in range(2):
            r = slice(b * DH, (b + 1) * DH)
            q = qg[0, r, hs(h)]
            p = dot(q, kv[0, r, hs(h)], 1, 1)
            p = jnp.where(mask, p, 0.0).astype(BF16)
            t = dot(p, kv[1, r, hs(h)], 1, 0)
            if b == 1:
                t = t + dot2(q, hi, lo, 0)
            intra[r, hs(h)] = t


def earlier_body(n, c, x, out):
    share = x.shape[0] // n
    acc = jnp.zeros((share, DH), F32)
    for i in range(n):
        out[i * share : (i + 1) * share, :] = acc
        if i + 1 < n:
            acc = acc + x[i * share : (i + 1) * share, :]


def attn_body(c, qg, intra, prior, gain, flat, parts):
    square = [jnp.zeros((DH, DH), F32) for _ in range(2)]
    cross = [jnp.zeros((DH, DH), F32) for _ in range(2)]
    for h in range(intra.shape[1] // DH):
        hi, lo = split(prior[hs(h), :])
        for b in range(2):
            r = slice(b * DH, (b + 1) * DH)
            f = intra[r, hs(h)] + dot2(qg[0, r, hs(h)], hi, lo, 0)
            flat[r, hs(h)] = f
            square[b] = square[b] + f * f
            cross[b] = cross[b] + (qg[1, r, hs(h)].astype(F32) * gain[:, hs(h)]) * f
    for b in range(2):
        sq = jnp.sum(square[b].T, axis=0, keepdims=True)
        cr = jnp.sum(cross[b].T, axis=0, keepdims=True)
        for j in range(parts.shape[0]):
            parts[j, b : b + 1, :] = sq
            parts[j, 2 + b : 3 + b, :] = cr


def grad_body(n, width, c, qg, flat, gain, parts, gd, out):
    heads = gd.shape[1] // DH
    own = heads * DH // n
    total = jnp.sum(parts[...], axis=0)
    gain_rows = [jnp.zeros((1, DH), F32) for _ in range(heads)]
    sums = [None] * heads
    for b in range(2):
        r = slice(b * DH, (b + 1) * DH)
        inverse = lax.rsqrt(total[b : b + 1, :] / width + EPS)
        scale = inverse * total[2 + b : 3 + b, :] / width
        inverse = jnp.broadcast_to(inverse, (DH, DH)).T
        scale = jnp.broadcast_to(scale, (DH, DH)).T
        for h in range(heads):
            g = qg[1, r, hs(h)].astype(F32)
            normed = flat[r, hs(h)] * inverse
            d = inverse * (g * gain[:, hs(h)] - normed * scale)
            gd[r, hs(h)] = d
            gain_rows[h] = gain_rows[h] + jnp.sum(g * normed, axis=0, keepdims=True)
            hi, lo = split(d)
            q = qg[0, r, hs(h)]
            s = dot(q, lo, 0, 0) + dot(q, hi, 0, 0)
            sums[h] = s if b == 0 else sums[h] + s
    for j in range(n):
        h, at = divmod(j * own, DH)
        out[j * (own + 1) : j * (own + 1) + own, :] = sums[h][at : at + own, :]
        out[j * (own + 1) + own : (j + 1) * (own + 1), :] = gain_rows[j % heads]


def query_body(c, qg, kv, gd, prior, keepq, keep, send, all3):
    mask = causal()
    for h in range(gd.shape[1] // DH):
        first = first_state(kv, h)
        second = None
        for b in (1, 0):
            r = slice(b * DH, (b + 1) * DH)
            q, k, v = qg[0, r, hs(h)], kv[0, r, hs(h)], kv[1, r, hs(h)]
            hi, lo = split(gd[r, hs(h)])
            p = dot(q, k, 1, 1)
            p = jnp.where(mask, p, 0.0).astype(BF16)
            dp = dot(hi, v, 1, 1)
            dp = jnp.where(mask, dp, 0.0).astype(BF16)
            prior_b = prior[hs(h), :]
            if b == 1:
                prior_b = prior_b + first
            phi, plo = split(prior_b)
            t = dot(lo, phi, 1, 1) + dot2(hi, phi, plo, 1)
            all3[0, r, hs(h)] = dot(dp, k, 1, 0) + t
            dk = dot(dp, q, 0, 0)
            dv = dot(p, hi, 0, 0)
            if b == 1:
                second = split(dot(q, lo, 0, 0) + dot(q, hi, 0, 0))
            else:
                dk = dk + dot2(v, *second, 1)
                dv = dv + dot2(k, *second, 0)
            all3[1, r, hs(h)] = dk
            all3[2, r, hs(h)] = dv
    mine = pl.multiple_of(c[0] * DH, DH)
    other = pl.multiple_of((1 - c[0]) * DH, DH)
    keepq[...] = all3[0, pl.ds(mine, DH), :].astype(BF16)
    keep[...] = all3[1:3, pl.ds(mine, DH), :]
    send[...] = all3[:, pl.ds(other, DH), :]


def later_body(n, c, x, out):
    share = x.shape[0] // n
    own = share - 1
    acc = jnp.zeros((own, DH), F32)
    gain = jnp.zeros((1, DH), F32)
    for i in range(n):
        gain = gain + x[i * share + own : (i + 1) * share, :]
    for i in reversed(range(n)):
        out[i * share : i * share + own, :] = acc
        out[i * share + own : (i + 1) * share, :] = gain
        if i:
            acc = acc + x[i * share : i * share + own, :]


def final_body(n, c, k, v, keepq, keep, early, mine, other, gq, gk, gv, gain):
    half = keep.shape[2]
    own = half // n
    per = DH // own

    def put(at, away):
        gq[:, at : at + half] = keepq[...]
        gq[:, away : away + half] = early[0].astype(BF16)
        for base, sums, part, i in ((at, mine, keep, 0), (away, other, early, 1)):
            for h in range(half // DH):
                to = slice(base + h * DH, base + (h + 1) * DH)
                later = [
                    sums[j * (own + 1) : j * (own + 1) + own, :]
                    for j in range(h * per, (h + 1) * per)
                ]
                hi, lo = split(jnp.concatenate(later, 0))
                dk = part[i, :, hs(h)] + dot2(v[:, to], hi, lo, 1)
                dv = part[i + 1, :, hs(h)] + dot2(k[:, to], hi, lo, 0)
                gk[:, to] = dk.astype(BF16)
                gv[:, to] = dv.astype(BF16)
                gain[:, to] = sums[h * (own + 1) + own : (h + 1) * (own + 1), :]

    @pl.when(c[0] == 0)
    def _():
        put(0, half)

    @pl.when(c[0] == 1)
    def _():
        put(half, 0)


def shards(query_rows, key_rows, value_rows, grad_output, norm_gain):
    count, width = query_rows.shape
    half = width // 2
    heads = half // DH
    both = 2 * count
    chips = lax.axis_size("chip")
    columns = lax.axis_size("head")
    full = columns * width
    at = lax.axis_index("core")
    core = at.astype(jnp.int32).reshape(1)
    swap = [(0, 1), (1, 0)]
    args = (query_rows, key_rows, value_rows, grad_output)
    gains = norm_gain.reshape(1, width)
    act = sds((both, half), F32)
    pair = sds((2, both, half), BF16)
    flat_state = sds((heads * DH, DH), F32)
    padded = sds((heads * DH + chips, DH), F32)

    def exchange(x):
        y = lax.all_to_all(
            x.reshape(chips, 1, -1), "chip", split_axis=0, concat_axis=0, tiled=True
        )
        return y.reshape(x.shape)

    sent = pl.pallas_call(
        send_body,
        name="send",
        out_shape=pltpu.VMEM((4, count, half), F32),
        grid_spec=pltpu.PrefetchScalarGridSpec(
            num_scalar_prefetch=1,
            grid=(1,),
            in_specs=[pl.BlockSpec((count, half), lambda i, c: (0, 1 - c[0]))] * 4,
            out_specs=pl.BlockSpec(memory_space=pltpu.VMEM),
        ),
    )(core, *args)
    got = lax.ppermute(sent, "core", swap)
    qg, kv, total = call("state", state_body, core, (*args, got), [pair, pair, flat_state])
    mine_states = exchange(total)
    intra, my_gain = call(
        "local", local_body, core, (qg, kv, gains), [act, sds((1, half), F32)]
    )
    sums = call(
        "earlier", functools.partial(earlier_body, chips), core, (mine_states,), [flat_state]
    )[0]
    prior = exchange(sums)
    flat, parts = call(
        "attn", attn_body, core, (qg, intra, prior, my_gain),
        [act, sds((2 * columns, 4, DH), F32)],
    )
    parts = lax.all_to_all(parts, ("core", "head"), split_axis=0, concat_axis=0, tiled=True)
    gd, block = call(
        "grad", functools.partial(grad_body, chips, full), core, (qg, flat, my_gain, parts),
        [act, padded],
    )
    mine_grads = exchange(block)
    keepq, keep, send = call(
        "query", query_body, core, (qg, kv, gd, prior),
        [sds((count, half), BF16), sds((2, count, half), F32), sds((3, count, half), F32)],
        scratch=[pltpu.VMEM((3, both, half), F32)],
    )
    early = lax.ppermute(send, "core", swap)
    later_sums = call(
        "later", functools.partial(later_body, chips), core, (mine_grads,), [padded]
    )[0]
    later = exchange(later_sums)
    others = lax.ppermute(later, "core", swap)
    gq, gk, gv, gain = call(
        "final", functools.partial(final_body, chips), core,
        (key_rows, value_rows, keepq, keep, early, later, others),
        [sds((count, width), BF16)] * 3 + [sds((1, width), F32)], far=(7, 8, 9, 10),
    )
    return gq, gk, gv, gain.reshape(width)


def solution(mesh):
    names = dict(mesh.shape)
    inner = Mesh(
        mesh.devices.reshape(names["seq"] // 2, 2, names["head"]), ("chip", "core", "head")
    )
    seq = ("chip", "core")
    placed = (P(seq, "head"),) * 4 + (P("head"),)
    return jax.shard_map(
        shards,
        mesh=inner,
        in_specs=placed,
        out_specs=(P(seq, "head"),) * 3 + (P("head"),),
        check_vma=False,
    )
```

```python
import functools

import jax
import jax.numpy as jnp
from jax import lax
from jax.experimental import pallas as pl
from jax.experimental.pallas import tpu as pltpu
from jax.sharding import Mesh, PartitionSpec as P


DH = 128
EPS = 1e-06
F32 = jnp.float32
BF16 = jnp.bfloat16


def dot(a, b, ca, cb):
    return lax.dot_general(a, b, (((ca,), (cb,)), ((), ())), preferred_element_type=F32)


def split(x):
    hi = x.astype(BF16)
    return hi, (x - hi.astype(F32)).astype(BF16)


def dot2(a, hi, lo, cb):
    return dot(jnp.concatenate([a, a], 1), jnp.concatenate([hi, lo], cb), 1, cb)


def causal():
    rows = lax.broadcasted_iota(jnp.int32, (DH, DH), 0)
    cols = lax.broadcasted_iota(jnp.int32, (DH, DH), 1)
    return rows >= cols


def hs(h):
    return slice(h * DH, (h + 1) * DH)


def call(body, core, ins, outs, scratch=(), far=()):
    vmem = pl.BlockSpec(memory_space=pltpu.VMEM)
    count = len(ins)
    ins = [
        x if i in far else pltpu.with_memory_space_constraint(x, pltpu.VMEM)
        for i, x in enumerate(ins)
    ]
    outs = [
        o if count + i in far else pltpu.VMEM(o.shape, o.dtype) for i, o in enumerate(outs)
    ]
    return pl.pallas_call(
        body,
        out_shape=outs,
        in_specs=[pl.BlockSpec(memory_space=pltpu.SMEM)] + [vmem] * len(ins),
        out_specs=[vmem] * len(outs),
        scratch_shapes=list(scratch),
        compiler_params=pltpu.CompilerParams(vmem_limit_bytes=16 * 2**20),
    )(core, *ins)


def windowed(body, core, ins, in_specs, outs):
    return pl.pallas_call(
        body,
        out_shape=[pltpu.VMEM(o.shape, o.dtype) for o in outs],
        grid_spec=pltpu.PrefetchScalarGridSpec(
            num_scalar_prefetch=1,
            grid=(1,),
            in_specs=in_specs,
            out_specs=[pl.BlockSpec(memory_space=pltpu.VMEM)] * len(outs),
        ),
    )(core, *ins)


def sds(shape, dtype):
    return jax.ShapeDtypeStruct(shape, dtype)


def half_of(ref, at, half):
    return ref[:, pl.ds(pl.multiple_of(at * half, DH), half)]


def send_body(c, q, k, v, g, out):
    for i, ref in enumerate((q, k, v, g)):
        out[i] = ref[...].astype(F32)


def state_body(c, k, v, mine, send):
    heads = mine.shape[0] // DH
    for out, at in ((mine, c[0]), (send, 1 - c[0])):
        for h in range(heads):
            to = pl.ds(pl.multiple_of((at * heads + h) * DH, DH), DH)
            out[hs(h), :] = dot(k[:, to], v[:, to], 0, 0)


def place_body(c, q, k, v, g, got, qg, kv):
    mine = pl.multiple_of(c[0] * DH, DH)
    other = pl.multiple_of((1 - c[0]) * DH, DH)
    for i, (ref, out, at) in enumerate(((q, qg, 0), (k, kv, 0), (v, kv, 1), (g, qg, 1))):
        out[at, pl.ds(mine, DH), :] = ref[...]
        out[at, pl.ds(other, DH), :] = got[i].astype(BF16)


def first_state(kv, h):
    return dot(kv[0, 0:DH, hs(h)], kv[1, 0:DH, hs(h)], 0, 0)


def local_body(c, qg, kv, gain, intra, my_gain):
    my_gain[...] = half_of(gain, c[0], my_gain.shape[1])
    mask = causal()
    for h in range(intra.shape[1] // DH):
        hi, lo = split(first_state(kv, h))
        for b in range(2):
            r = slice(b * DH, (b + 1) * DH)
            q = qg[0, r, hs(h)]
            p = dot(q, kv[0, r, hs(h)], 1, 1)
            p = jnp.where(mask, p, 0.0).astype(BF16)
            t = dot(p, kv[1, r, hs(h)], 1, 0)
            if b == 1:
                t = t + dot2(q, hi, lo, 0)
            intra[r, hs(h)] = t


def earlier_body(n, c, x, after, out):
    share = x.shape[0] // n
    acc = jnp.zeros((share, DH), F32)
    for i in range(n):
        out[i * share : (i + 1) * share, :] = acc
        if i + 1 < n:
            acc = acc + x[i * share : (i + 1) * share, :]


def attn_body(c, qg, intra, prior, gain, flat, parts):
    square = [jnp.zeros((DH, DH), F32) for _ in range(2)]
    cross = [jnp.zeros((DH, DH), F32) for _ in range(2)]
    for h in range(intra.shape[1] // DH):
        hi, lo = split(prior[hs(h), :])
        for b in range(2):
            r = slice(b * DH, (b + 1) * DH)
            f = intra[r, hs(h)] + dot2(qg[0, r, hs(h)], hi, lo, 0)
            flat[r, hs(h)] = f
            square[b] = square[b] + f * f
            cross[b] = cross[b] + (qg[1, r, hs(h)].astype(F32) * gain[:, hs(h)]) * f
    for b in range(2):
        sq = jnp.sum(square[b].T, axis=0, keepdims=True)
        cr = jnp.sum(cross[b].T, axis=0, keepdims=True)
        for j in range(parts.shape[0]):
            parts[j, b : b + 1, :] = sq
            parts[j, 2 + b : 3 + b, :] = cr


def grad_body(n, width, c, qg, flat, gain, parts, gd, out):
    heads = gd.shape[1] // DH
    own = heads * DH // n
    total = jnp.sum(parts[...], axis=0)
    gain_rows = [jnp.zeros((1, DH), F32) for _ in range(heads)]
    sums = [None] * heads
    for b in range(2):
        r = slice(b * DH, (b + 1) * DH)
        inverse = lax.rsqrt(total[b : b + 1, :] / width + EPS)
        scale = inverse * total[2 + b : 3 + b, :] / width
        inverse = jnp.broadcast_to(inverse, (DH, DH)).T
        scale = jnp.broadcast_to(scale, (DH, DH)).T
        for h in range(heads):
            g = qg[1, r, hs(h)].astype(F32)
            normed = flat[r, hs(h)] * inverse
            d = inverse * (g * gain[:, hs(h)] - normed * scale)
            gd[r, hs(h)] = d
            gain_rows[h] = gain_rows[h] + jnp.sum(g * normed, axis=0, keepdims=True)
            hi, lo = split(d)
            q = qg[0, r, hs(h)]
            s = dot(q, lo, 0, 0) + dot(q, hi, 0, 0)
            sums[h] = s if b == 0 else sums[h] + s
    for j in range(n):
        h, at = divmod(j * own, DH)
        out[j * (own + 1) : j * (own + 1) + own, :] = sums[h][at : at + own, :]
        out[j * (own + 1) + own : (j + 1) * (own + 1), :] = gain_rows[j % heads]


def query_body(c, qg, kv, gd, prior, keepq, keep, send, all3):
    mask = causal()
    for h in range(gd.shape[1] // DH):
        first = first_state(kv, h)
        second = None
        for b in (1, 0):
            r = slice(b * DH, (b + 1) * DH)
            q, k, v = qg[0, r, hs(h)], kv[0, r, hs(h)], kv[1, r, hs(h)]
            hi, lo = split(gd[r, hs(h)])
            p = dot(q, k, 1, 1)
            p = jnp.where(mask, p, 0.0).astype(BF16)
            dp = dot(hi, v, 1, 1)
            dp = jnp.where(mask, dp, 0.0).astype(BF16)
            prior_b = prior[hs(h), :]
            if b == 1:
                prior_b = prior_b + first
            phi, plo = split(prior_b)
            t = dot(lo, phi, 1, 1) + dot2(hi, phi, plo, 1)
            all3[0, r, hs(h)] = dot(dp, k, 1, 0) + t
            dk = dot(dp, q, 0, 0)
            dv = dot(p, hi, 0, 0)
            if b == 1:
                second = split(dot(q, lo, 0, 0) + dot(q, hi, 0, 0))
            else:
                dk = dk + dot2(v, *second, 1)
                dv = dv + dot2(k, *second, 0)
            all3[1, r, hs(h)] = dk
            all3[2, r, hs(h)] = dv
    mine = pl.multiple_of(c[0] * DH, DH)
    other = pl.multiple_of((1 - c[0]) * DH, DH)
    keepq[...] = all3[0, pl.ds(mine, DH), :].astype(BF16)
    keep[...] = all3[1:3, pl.ds(mine, DH), :]
    send[...] = all3[:, pl.ds(other, DH), :]


def later_body(n, c, x, out):
    share = x.shape[0] // n
    own = share - 1
    acc = jnp.zeros((own, DH), F32)
    gain = jnp.zeros((1, DH), F32)
    for i in range(n):
        gain = gain + x[i * share + own : (i + 1) * share, :]
    for i in reversed(range(n)):
        out[i * share : i * share + own, :] = acc
        out[i * share + own : (i + 1) * share, :] = gain
        if i:
            acc = acc + x[i * share : i * share + own, :]


def final_body(n, c, k, v, keepq, keep, early, mine, other, gq, gk, gv, gain):
    half = keep.shape[2]
    own = half // n
    per = DH // own

    def put(at, away):
        gq[:, at : at + half] = keepq[...]
        gq[:, away : away + half] = early[0].astype(BF16)
        for base, sums, part, i in ((at, mine, keep, 0), (away, other, early, 1)):
            for h in range(half // DH):
                to = slice(base + h * DH, base + (h + 1) * DH)
                later = [
                    sums[j * (own + 1) : j * (own + 1) + own, :]
                    for j in range(h * per, (h + 1) * per)
                ]
                hi, lo = split(jnp.concatenate(later, 0))
                dk = part[i, :, hs(h)] + dot2(v[:, to], hi, lo, 1)
                dv = part[i + 1, :, hs(h)] + dot2(k[:, to], hi, lo, 0)
                gk[:, to] = dk.astype(BF16)
                gv[:, to] = dv.astype(BF16)
                gain[:, to] = sums[h * (own + 1) + own : (h + 1) * (own + 1), :]

    @pl.when(c[0] == 0)
    def _():
        put(0, half)

    @pl.when(c[0] == 1)
    def _():
        put(half, 0)


def shards(query_rows, key_rows, value_rows, grad_output, norm_gain):
    count, width = query_rows.shape
    half = width // 2
    heads = half // DH
    both = 2 * count
    chips = lax.axis_size("chip")
    columns = lax.axis_size("head")
    full = columns * width
    at = lax.axis_index("core")
    core = at.astype(jnp.int32).reshape(1)
    swap = [(0, 1), (1, 0)]
    args = (query_rows, key_rows, value_rows, grad_output)
    gains = norm_gain.reshape(1, width)
    act = sds((both, half), F32)
    pair = sds((2, both, half), BF16)
    flat_state = sds((heads * DH, DH), F32)
    padded = sds((heads * DH + chips, DH), F32)

    def exchange(x):
        y = lax.all_to_all(
            x.reshape(chips, 1, -1), "chip", split_axis=0, concat_axis=0, tiled=True
        )
        return y.reshape(x.shape)

    all_cols = pl.BlockSpec((count, width), lambda i, c: (0, 0))
    my_cols = pl.BlockSpec((count, half), lambda i, c: (0, c[0]))
    away_cols = pl.BlockSpec((count, half), lambda i, c: (0, 1 - c[0]))
    own, send = windowed(state_body, core, (key_rows, value_rows), [all_cols] * 2, [flat_state] * 2)
    total = own + lax.ppermute(send, "core", swap)
    mine_states = exchange(total)
    sent = windowed(send_body, core, args, [away_cols] * 4, [sds((4, count, half), F32)])[0]
    got = lax.ppermute(sent, "core", swap)
    qg, kv = windowed(
        place_body, core,
        (*args, got), [my_cols] * 4 + [pl.BlockSpec(got.shape, lambda i, c: (0, 0, 0))],
        [pair, pair],
    )
    intra, my_gain = call(local_body, core, (qg, kv, gains), [act, sds((1, half), F32)])
    sums = call(functools.partial(earlier_body, chips), core, (mine_states, qg), [flat_state])[0]
    prior = exchange(sums)
    flat, parts = call(
        attn_body, core, (qg, intra, prior, my_gain),
        [act, sds((2 * columns, 4, DH), F32)],
    )
    parts = lax.all_to_all(parts, ("core", "head"), split_axis=0, concat_axis=0, tiled=True)
    gd, block = call(
        functools.partial(grad_body, chips, full), core, (qg, flat, my_gain, parts),
        [act, padded],
    )
    mine_grads = exchange(block)
    keepq, keep, send = call(
        query_body, core, (qg, kv, gd, prior),
        [sds((count, half), BF16), sds((2, count, half), F32), sds((3, count, half), F32)],
        scratch=[pltpu.VMEM((3, both, half), F32)],
    )
    early = lax.ppermute(send, "core", swap)
    later_sums = call(functools.partial(later_body, chips), core, (mine_grads,), [padded])[0]
    later = exchange(later_sums)
    others = lax.ppermute(later, "core", swap)
    gq, gk, gv, gain = call(
        functools.partial(final_body, chips), core,
        (key_rows, value_rows, keepq, keep, early, later, others),
        [sds((count, width), BF16)] * 3 + [sds((1, width), F32)], far=(7, 8, 9, 10),
    )
    return gq, gk, gv, gain.reshape(width)


def solution(mesh):
    names = dict(mesh.shape)
    inner = Mesh(
        mesh.devices.reshape(names["seq"] // 2, 2, names["head"]), ("chip", "core", "head")
    )
    seq = ("chip", "core")
    placed = (P(seq, "head"),) * 4 + (P("head"),)
    return jax.shard_map(
        shards,
        mesh=inner,
        in_specs=placed,
        out_specs=(P(seq, "head"),) * 3 + (P("head"),),
        check_vma=False,
    )
```

```python
import functools

import jax
import jax.numpy as jnp
from jax import lax
from jax.experimental import pallas as pl
from jax.experimental.pallas import tpu as pltpu
from jax.sharding import Mesh, PartitionSpec as P


DH = 128
EPS = 1e-06
F32 = jnp.float32
BF16 = jnp.bfloat16


def dot(a, b, ca, cb):
    return lax.dot_general(a, b, (((ca,), (cb,)), ((), ())), preferred_element_type=F32)


def split(x):
    hi = x.astype(BF16)
    return hi, (x - hi.astype(F32)).astype(BF16)


def dot2(a, hi, lo, cb):
    return dot(jnp.concatenate([a, a], 1), jnp.concatenate([hi, lo], cb), 1, cb)


def causal():
    rows = lax.broadcasted_iota(jnp.int32, (DH, DH), 0)
    cols = lax.broadcasted_iota(jnp.int32, (DH, DH), 1)
    return rows >= cols


def hs(h):
    return slice(h * DH, (h + 1) * DH)


def call(body, core, ins, outs, scratch=(), far=()):
    vmem = pl.BlockSpec(memory_space=pltpu.VMEM)
    count = len(ins)
    ins = [
        x if i in far else pltpu.with_memory_space_constraint(x, pltpu.VMEM)
        for i, x in enumerate(ins)
    ]
    outs = [
        o if count + i in far else pltpu.VMEM(o.shape, o.dtype) for i, o in enumerate(outs)
    ]
    return pl.pallas_call(
        body,
        out_shape=outs,
        in_specs=[pl.BlockSpec(memory_space=pltpu.SMEM)] + [vmem] * len(ins),
        out_specs=[vmem] * len(outs),
        scratch_shapes=list(scratch),
        compiler_params=pltpu.CompilerParams(vmem_limit_bytes=16 * 2**20),
    )(core, *ins)


def sds(shape, dtype):
    return jax.ShapeDtypeStruct(shape, dtype)


def half_of(ref, at, half):
    return ref[:, pl.ds(pl.multiple_of(at * half, DH), half)]


def send_body(c, a, b, out):
    out[0] = a[...].astype(F32)
    out[1] = b[...].astype(F32)


def place(c, ref, got, row, out, at):
    mine = pl.multiple_of(c[0] * DH, DH)
    other = pl.multiple_of((1 - c[0]) * DH, DH)
    out[at, pl.ds(mine, DH), :] = half_of(ref, c[0], out.shape[2])
    out[at, pl.ds(other, DH), :] = got[row].astype(BF16)


def state_body(c, k, v, got, kv, total):
    place(c, k, got, 0, kv, 0)
    place(c, v, got, 1, kv, 1)
    for h in range(total.shape[0] // DH):
        total[hs(h), :] = dot(kv[0, :, hs(h)], kv[1, :, hs(h)], 0, 0)


def first_state(kv, h):
    return dot(kv[0, 0:DH, hs(h)], kv[1, 0:DH, hs(h)], 0, 0)


def local_body(c, q, g, got, kv, gain, qg, intra, my_gain):
    place(c, q, got, 0, qg, 0)
    place(c, g, got, 1, qg, 1)
    my_gain[...] = half_of(gain, c[0], my_gain.shape[1])
    mask = causal()
    for h in range(intra.shape[1] // DH):
        hi, lo = split(first_state(kv, h))
        for b in range(2):
            r = slice(b * DH, (b + 1) * DH)
            query = qg[0, r, hs(h)]
            p = dot(query, kv[0, r, hs(h)], 1, 1)
            p = jnp.where(mask, p, 0.0).astype(BF16)
            t = dot(p, kv[1, r, hs(h)], 1, 0)
            if b == 1:
                t = t + dot2(query, hi, lo, 0)
            intra[r, hs(h)] = t


def earlier_body(n, c, x, out):
    share = x.shape[0] // n
    acc = jnp.zeros((share, DH), F32)
    for i in range(n):
        out[i * share : (i + 1) * share, :] = acc
        if i + 1 < n:
            acc = acc + x[i * share : (i + 1) * share, :]


def attn_body(c, qg, intra, prior, gain, flat, parts):
    square = [jnp.zeros((DH, DH), F32) for _ in range(2)]
    cross = [jnp.zeros((DH, DH), F32) for _ in range(2)]
    for h in range(intra.shape[1] // DH):
        hi, lo = split(prior[hs(h), :])
        for b in range(2):
            r = slice(b * DH, (b + 1) * DH)
            f = intra[r, hs(h)] + dot2(qg[0, r, hs(h)], hi, lo, 0)
            flat[r, hs(h)] = f
            square[b] = square[b] + f * f
            cross[b] = cross[b] + (qg[1, r, hs(h)].astype(F32) * gain[:, hs(h)]) * f
    for b in range(2):
        sq = jnp.sum(square[b].T, axis=0, keepdims=True)
        cr = jnp.sum(cross[b].T, axis=0, keepdims=True)
        for j in range(parts.shape[0]):
            parts[j, b : b + 1, :] = sq
            parts[j, 2 + b : 3 + b, :] = cr


def grad_body(n, width, c, qg, flat, gain, parts, gd, out):
    heads = gd.shape[1] // DH
    own = heads * DH // n
    total = jnp.sum(parts[...], axis=0)
    gain_rows = [jnp.zeros((1, DH), F32) for _ in range(heads)]
    sums = [None] * heads
    for b in range(2):
        r = slice(b * DH, (b + 1) * DH)
        inverse = lax.rsqrt(total[b : b + 1, :] / width + EPS)
        scale = inverse * total[2 + b : 3 + b, :] / width
        inverse = jnp.broadcast_to(inverse, (DH, DH)).T
        scale = jnp.broadcast_to(scale, (DH, DH)).T
        for h in range(heads):
            g = qg[1, r, hs(h)].astype(F32)
            normed = flat[r, hs(h)] * inverse
            d = inverse * (g * gain[:, hs(h)] - normed * scale)
            gd[r, hs(h)] = d
            gain_rows[h] = gain_rows[h] + jnp.sum(g * normed, axis=0, keepdims=True)
            hi, lo = split(d)
            q = qg[0, r, hs(h)]
            s = dot(q, lo, 0, 0) + dot(q, hi, 0, 0)
            sums[h] = s if b == 0 else sums[h] + s
    for j in range(n):
        h, at = divmod(j * own, DH)
        out[j * (own + 1) : j * (own + 1) + own, :] = sums[h][at : at + own, :]
        out[j * (own + 1) + own : (j + 1) * (own + 1), :] = gain_rows[j % heads]


def query_body(c, qg, kv, gd, prior, keepq, keep, send, all3):
    mask = causal()
    for h in range(gd.shape[1] // DH):
        first = first_state(kv, h)
        second = None
        for b in (1, 0):
            r = slice(b * DH, (b + 1) * DH)
            q, k, v = qg[0, r, hs(h)], kv[0, r, hs(h)], kv[1, r, hs(h)]
            hi, lo = split(gd[r, hs(h)])
            p = dot(q, k, 1, 1)
            p = jnp.where(mask, p, 0.0).astype(BF16)
            dp = dot(hi, v, 1, 1)
            dp = jnp.where(mask, dp, 0.0).astype(BF16)
            prior_b = prior[hs(h), :]
            if b == 1:
                prior_b = prior_b + first
            phi, plo = split(prior_b)
            t = dot(lo, phi, 1, 1) + dot2(hi, phi, plo, 1)
            all3[0, r, hs(h)] = dot(dp, k, 1, 0) + t
            dk = dot(dp, q, 0, 0)
            dv = dot(p, hi, 0, 0)
            if b == 1:
                second = split(dot(q, lo, 0, 0) + dot(q, hi, 0, 0))
            else:
                dk = dk + dot2(v, *second, 1)
                dv = dv + dot2(k, *second, 0)
            all3[1, r, hs(h)] = dk
            all3[2, r, hs(h)] = dv
    mine = pl.multiple_of(c[0] * DH, DH)
    other = pl.multiple_of((1 - c[0]) * DH, DH)
    keepq[...] = all3[0, pl.ds(mine, DH), :].astype(BF16)
    keep[...] = all3[1:3, pl.ds(mine, DH), :]
    send[...] = all3[:, pl.ds(other, DH), :]


def later_body(n, c, x, out):
    share = x.shape[0] // n
    own = share - 1
    acc = jnp.zeros((own, DH), F32)
    gain = jnp.zeros((1, DH), F32)
    for i in range(n):
        gain = gain + x[i * share + own : (i + 1) * share, :]
    for i in reversed(range(n)):
        out[i * share : i * share + own, :] = acc
        out[i * share + own : (i + 1) * share, :] = gain
        if i:
            acc = acc + x[i * share : i * share + own, :]


def finish(n, k, v, sums, dk, dv, gk, gv, gain):
    half = gk.shape[1]
    own = half // n
    per = DH // own
    for h in range(half // DH):
        later = [
            sums[j * (own + 1) : j * (own + 1) + own, :]
            for j in range(h * per, (h + 1) * per)
        ]
        hi, lo = split(jnp.concatenate(later, 0))
        gk[:, hs(h)] = (dk[:, hs(h)] + dot2(v[:, hs(h)], hi, lo, 1)).astype(BF16)
        gv[:, hs(h)] = (dv[:, hs(h)] + dot2(k[:, hs(h)], hi, lo, 0)).astype(BF16)
        gain[:, hs(h)] = sums[h * (own + 1) + own : (h + 1) * (own + 1), :]


def mine_body(n, c, k, v, keepq, keep, sums, gq, gk, gv, gain):
    half = gq.shape[1]
    gq[...] = keepq[...]
    k, v = half_of(k, c[0], half), half_of(v, c[0], half)
    finish(n, k, v, sums, keep[0], keep[1], gk, gv, gain)


def away_body(n, c, k, v, early, sums, q0, k0, v0, g0, gq, gk, gv, gain):
    half = gq.shape[1]
    gq[...] = early[0].astype(BF16)
    k, v = half_of(k, 1 - c[0], half), half_of(v, 1 - c[0], half)
    finish(n, k, v, sums, early[1], early[2], gk, gv, gain)


def shards(query_rows, key_rows, value_rows, grad_output, norm_gain):
    count, width = query_rows.shape
    half = width // 2
    heads = half // DH
    both = 2 * count
    chips = lax.axis_size("chip")
    columns = lax.axis_size("head")
    full = columns * width
    at = lax.axis_index("core")
    core = at.astype(jnp.int32).reshape(1)
    swap = [(0, 1), (1, 0)]
    gains = norm_gain.reshape(1, width)
    act = sds((both, half), F32)
    pair = sds((2, both, half), BF16)
    flat_state = sds((heads * DH, DH), F32)
    padded = sds((heads * DH + chips, DH), F32)

    def exchange(x):
        y = lax.all_to_all(
            x.reshape(chips, 1, -1), "chip", split_axis=0, concat_axis=0, tiled=True
        )
        return y.reshape(x.shape)

    away_cols = pl.BlockSpec((count, half), lambda i, c: (0, 1 - c[0]))

    def swapped(*pair_of):
        sent = pl.pallas_call(
            send_body,
            name="send",
            out_shape=[pltpu.VMEM((2, count, half), F32)],
            grid_spec=pltpu.PrefetchScalarGridSpec(
                num_scalar_prefetch=1,
                grid=(1,),
                in_specs=[away_cols] * 2,
                out_specs=[pl.BlockSpec(memory_space=pltpu.VMEM)],
            ),
        )(core, *pair_of)[0]
        return lax.ppermute(sent, "core", swap)

    got = swapped(key_rows, value_rows)
    kv, total = call(state_body, core, (key_rows, value_rows, got), [pair, flat_state])
    mine_states = exchange(total)
    got = swapped(query_rows, grad_output)
    qg, intra, my_gain = call(
        local_body, core, (query_rows, grad_output, got, kv, gains),
        [pair, act, sds((1, half), F32)],
    )
    sums = call(functools.partial(earlier_body, chips), core, (mine_states,), [flat_state])[0]
    prior = exchange(sums)
    flat, parts = call(
        attn_body, core, (qg, intra, prior, my_gain),
        [act, sds((2 * columns, 4, DH), F32)],
    )
    parts = lax.all_to_all(parts, ("core", "head"), split_axis=0, concat_axis=0, tiled=True)
    gd, block = call(
        functools.partial(grad_body, chips, full), core, (qg, flat, my_gain, parts),
        [act, padded],
    )
    mine_grads = exchange(block)
    keepq, keep, send = call(
        query_body, core, (qg, kv, gd, prior),
        [sds((count, half), BF16), sds((2, count, half), F32), sds((3, count, half), F32)],
        scratch=[pltpu.VMEM((3, both, half), F32)],
    )
    early = lax.ppermute(send, "core", swap)
    later_sums = call(functools.partial(later_body, chips), core, (mine_grads,), [padded])[0]
    later = exchange(later_sums)
    others = lax.ppermute(later, "core", swap)
    outs = [sds((count, width), BF16)] * 3 + [sds((1, width), F32)]
    vmem = pl.BlockSpec(memory_space=pltpu.VMEM)

    def final(body, at, ins, before=()):
        ins = [pltpu.with_memory_space_constraint(x, pltpu.VMEM) for x in ins]
        return pl.pallas_call(
            functools.partial(body, chips),
            out_shape=outs,
            grid_spec=pltpu.PrefetchScalarGridSpec(
                num_scalar_prefetch=1,
                grid=(1,),
                in_specs=[vmem] * len(ins) + [pl.BlockSpec(memory_space=pl.ANY)] * len(before),
                out_specs=[pl.BlockSpec((count, half), lambda i, c: (0, at(c[0])))] * 3
                + [pl.BlockSpec((1, half), lambda i, c: (0, at(c[0])))],
            ),
            input_output_aliases={1 + len(ins) + i: i for i in range(len(before))},
            compiler_params=pltpu.CompilerParams(vmem_limit_bytes=16 * 2**20),
        )(core, *ins, *before)

    before = final(mine_body, lambda x: x, (key_rows, value_rows, keepq, keep, later))
    gq, gk, gv, gain = final(
        away_body, lambda x: 1 - x, (key_rows, value_rows, early, others), before
    )
    return gq, gk, gv, gain.reshape(width)


def solution(mesh):
    names = dict(mesh.shape)
    inner = Mesh(
        mesh.devices.reshape(names["seq"] // 2, 2, names["head"]), ("chip", "core", "head")
    )
    seq = ("chip", "core")
    placed = (P(seq, "head"),) * 4 + (P("head"),)
    return jax.shard_map(
        shards,
        mesh=inner,
        in_specs=placed,
        out_specs=(P(seq, "head"),) * 3 + (P("head"),),
        check_vma=False,
    )
```
